512 devices in a mesh: expert: 32 (over x, y, core), tensor: 16 (over z).
Axes of the slice: x: 4, y: 4, z: 16, core: 2. Of those that a mesh axis runs over, the one named last changes fastest.
Arguments:
- tokens: bfloat16 [1024, 7168], P('expert', 'tensor'), may hold values from -6 to 6
- expert_ids: int32 [1024, 8], P('expert'), may hold values from 0 to 31, all different within a row; in each aligned block of 32 rows (0 to 31, 32 to 63, ...) at most 24 rows name the same one
- combine: float32 [1024, 8], P('expert'), may hold values from 0.1 to 0.5
- w_in: bfloat16 [32, 7168, 2048], P('expert', None, 'tensor'), may hold values from -0.0625 to 0.0625
- w_down: bfloat16 [32, 1024, 7168], P('expert', None, 'tensor'), may hold values from -0.1875 to 0.1875
Outputs:
- moe_out: bfloat16 [1024, 7168], P('expert', 'tensor')
The draws below stay inside these ranges and needn't reach their ends.
Inputs may be any that keep to these rules, and one draw needn't show every extreme that they name: `expert_ids`: each row names 8 different experts. Within the 32 tokens of one index of expert, no expert is named by more than 24 rows.
All inputs are finite; a program needn't handle non-finite values.
Results may differ from the reference program's by a relative error of at most 0.008.
Values may be sent and summed in bfloat16 or wider, within the bound.
No kernel may reach another device: no remote copies, remote signals or barrier semaphores. Data moves between devices by JAX's collectives and lax.ppermute only.
A program may use at most 64 MiB of HBM per device.

```python
import math
import jax
import jax.numpy as jnp
import numpy as np
from jax import lax

D = 7168
HID = 1024
TOP = 8
TOK_G = 32
EXPERTS = 32
TOKENS = 1024
CAP = 24
N_EXPERT = 32
N_TENSOR = 16


def shard_levels(stream_key, shape, split, smallest, largest):
    factor_of = 1.0
    for dim, blocks in split:
        draws = jax.random.uniform(jax.random.fold_in(jax.random.fold_in(stream_key, 6), dim), (blocks,), jnp.float32, smallest / len(split), largest / len(split))
        factor_of = factor_of * jnp.repeat(jnp.exp(draws), shape[dim] // blocks).reshape((-1,) + (1,) * (len(shape) - 1 - dim))
    return factor_of


def assign_block(own_key, own, number, rows, count, top, most, slope):
    order = jax.random.permutation(own_key, count)
    packed, ordinary = shares(count, rows * top, most, slope, True), shares(count, rows * top, most, slope, False)
    places = jnp.arange(count)

    def named(sizes, turn):
        used = int((sizes > 0).sum())
        fixed = max(1, used // 4)
        passed = fixed + (places - fixed + turn * (used - fixed)) % max(1, count - fixed)
        return jnp.zeros((count,), jnp.int32).at[order[jnp.where(places < fixed, places, passed)]].set(jnp.asarray(sizes, jnp.int32))

    sizes = jnp.where(number % 4 == 0, named(packed, number // 4), named(ordinary, number - number // 4 - 1))
    mixed = jax.random.permutation(jax.random.fold_in(own, 3), count)
    source_of, sink = mixed[0:count // 2 * 2:2], mixed[1:count // 2 * 2:2]
    room = jnp.minimum(sizes[source_of] - 1, most - sizes[sink]) // 2
    room = jnp.where((source_of == order[0]) | (sink == order[0]) | (sizes[sink] == 0), 0, jnp.maximum(room, 0))
    passed = jax.random.randint(jax.random.fold_in(own, 4), (count // 2,), 0, 1 << 20) % (room + 1)
    sizes = sizes.at[source_of].add(-passed).at[sink].add(passed)
    items = jnp.searchsorted(jnp.cumsum(sizes), jnp.arange(rows * top), side="right").astype(jnp.int32)
    grid = items.reshape(top, rows).T
    grid = grid[jax.random.permutation(jax.random.fold_in(own, 1), rows)]
    turn = jax.random.randint(jax.random.fold_in(own, 2), (rows, 1), 0, top)
    return jnp.take_along_axis(grid, (jnp.arange(top)[None, :] + turn) % top, axis=1)


def shares(count, total, reach, lean, full):
    weights = [(1 << 20) // math.isqrt(standing ** lean) + 1 for standing in range(1, count + 1)]
    largest = reach if full else min(reach, max(-(-total // count), total * weights[0] // sum(weights)))
    least = 1 if total - largest >= count - 1 else 0
    counts, surplus = [largest] + [least] * (count - 1), total - largest - least * (count - 1)
    while surplus > 0:
        movable = [i for i in range(1, count) if counts[i] < largest] or [i for i in range(1, count) if counts[i] < reach]
        mass, left = sum([weights[i] for i in movable]), surplus
        for i in movable:
            addition = min(reach - counts[i], max(1, left * weights[i] // mass), surplus)
            counts[i] = counts[i] + addition
            surplus = surplus - addition
    return np.array(counts)


def scatter_about(own_key, dims, spread, limit, pieces=(), kind=jnp.bfloat16):
    array = spread * jax.random.normal(own_key, dims, jnp.float32)
    if pieces:
        array = array * shard_levels(own_key, dims, pieces, -0.22, 0.18)
    return jnp.clip(array, -limit, limit).astype(kind)


def setup_inputs(seed: int = 0) -> dict:
    arg_keys = jax.random.split(jax.random.key(seed), 6)
    tokens = scatter_about(arg_keys[0], (TOKENS, D), 1.0, 6.0, ((0, 32), (1, 16)))
    expert_ids_keys = jax.random.split(jax.random.fold_in(arg_keys[1], 1), TOKENS // TOK_G)
    expert_ids_turns = jax.random.permutation(jax.random.fold_in(arg_keys[1], 3), TOKENS // TOK_G)
    expert_ids = jax.vmap(lambda own, number: assign_block(jax.random.fold_in(arg_keys[1], 2), own, number, TOK_G, EXPERTS, TOP, CAP, 2))(expert_ids_keys, expert_ids_turns).reshape((TOKENS, TOP))
    combine = jnp.clip(0.1 + 0.4 * jax.random.uniform(arg_keys[2], (TOKENS, TOP), jnp.float32) ** shard_levels(arg_keys[2], (TOKENS, TOP), ((0, 32),), -0.2, 0.2), 0.1, 0.5)
    w_in = scatter_about(arg_keys[3], (EXPERTS, D, 2 * HID), D ** -0.5, 0.0625, ((0, 32), (2, 16)))
    w_down = scatter_about(arg_keys[4], (EXPERTS, HID, D), HID ** -0.5, 0.1875, ((0, 32), (2, 16)))
    return dict(tokens=tokens, expert_ids=expert_ids, combine=combine, w_in=w_in, w_down=w_down)


def expert_apply(rows_in, gate_up_w, down_w):
    count_rows = rows_in.shape[0]
    gate_up = jnp.dot(rows_in, gate_up_w, preferred_element_type=jnp.float32)
    blocks = gate_up.reshape(count_rows, N_TENSOR, 2, HID // N_TENSOR)
    gate_part = blocks[:, :, 0, :].reshape(count_rows, HID)
    up_part = blocks[:, :, 1, :].reshape(count_rows, HID)
    hidden = (jax.nn.silu(gate_part) * up_part).astype(jnp.bfloat16)
    return jnp.dot(hidden, down_w, preferred_element_type=jnp.float32).astype(jnp.bfloat16)


def reference(tokens, expert_ids, combine, w_in, w_down):
    tok_group = TOKENS // N_EXPERT
    one_hot = (expert_ids[:, :, None] == jnp.arange(EXPERTS, dtype=jnp.int32)[None, None, :]).astype(jnp.int32)
    per_token = jnp.sum(one_hot, axis=1).reshape(N_EXPERT, tok_group, EXPERTS)
    before = (jnp.cumsum(per_token, axis=1) - per_token).reshape(TOKENS, EXPERTS)
    slot_index = jnp.take_along_axis(before, expert_ids, axis=1)
    source = (jnp.arange(TOKENS, dtype=jnp.int32) // tok_group)[:, None]
    position = source * CAP + slot_index
    buffer_rows = N_EXPERT * CAP
    flat_index = (expert_ids * buffer_rows + position).reshape(-1).astype(jnp.int32)
    token_index = jnp.repeat(jnp.arange(TOKENS, dtype=jnp.int32), TOP)
    table = jnp.full((EXPERTS * buffer_rows,), TOKENS, dtype=jnp.int32).at[flat_index].set(token_index)
    table = table.reshape(EXPERTS, buffer_rows)
    padded = jnp.concatenate([tokens, jnp.zeros((1, D), tokens.dtype)], axis=0)

    def one_expert(number):
        rows_in = padded[table[number]]
        return expert_apply(rows_in, w_in[number], w_down[number])

    outputs = lax.map(one_expert, jnp.arange(EXPERTS, dtype=jnp.int32))
    picked = outputs.reshape(EXPERTS * buffer_rows, D)[flat_index].reshape(TOKENS, TOP, D)
    summed = jnp.einsum("tk,tkd->td", combine.astype(jnp.float32), picked.astype(jnp.float32))
    return summed.astype(jnp.bfloat16)
```

```python
import functools

import jax
import jax.numpy as jnp
from jax import lax
from jax.experimental import pallas as pl
from jax.experimental.pallas import tpu as pltpu
from jax.sharding import Mesh, PartitionSpec as P


XY = ("x", "y")
PAD = 128


def gate_up_kernel(half_ref, rows_ref, wa0_ref, wb0_ref, wa1_ref, wb1_ref, out_ref, acc_ref):
    step = pl.program_id(0)

    @pl.when(step == 0)
    def _():
        acc_ref[...] = jnp.zeros_like(acc_ref)

    weights = jnp.concatenate([wa0_ref[...], wa1_ref[...], wb0_ref[...], wb1_ref[...]], axis=1)
    acc_ref[...] += jnp.dot(rows_ref[...], weights, preferred_element_type=jnp.float32)

    @pl.when(step == pl.num_programs(0) - 1)
    def _():
        lane = lax.broadcasted_iota(jnp.int32, (rows_ref.shape[0], 128), 1)
        low = lane < 64
        first = jnp.where(low, 0, 1) == half_ref[0]

        def hidden(at):
            value = acc_ref[:, at : at + 128]
            turned = pltpu.roll(value, 64, 1)
            gate = jnp.where(low, value, turned)
            up = jnp.where(low, turned, value)
            return gate / (1.0 + jnp.exp(-gate)) * up

        for e in range(2):
            both = jnp.where(first, hidden(256 * e), hidden(256 * e + 128))
            out_ref[:, 128 * e : 128 * e + 128] = both.astype(jnp.bfloat16)


def gate_up(half, rows, wa0, wb0, wa1, wb1, depth):
    count, chunk = rows.shape[0], 1024
    w_spec = pl.BlockSpec((chunk, 128), lambda k: (k, 0))
    return pl.pallas_call(
        gate_up_kernel,
        grid=(depth // chunk,),
        in_specs=[
            pl.BlockSpec(memory_space=pltpu.SMEM),
            pl.BlockSpec((count, chunk), lambda k: (0, k)),
            w_spec,
            w_spec,
            w_spec,
            w_spec,
        ],
        out_specs=pl.BlockSpec((count, 256), lambda k: (0, 0)),
        out_shape=jax.ShapeDtypeStruct((count, 256), jnp.bfloat16),
        scratch_shapes=[pltpu.VMEM((count, 512), jnp.float32)],
        name="gate_up",
    )(half, rows, wa0, wb0, wa1, wb1)


def down_kernel(half_ref, hidden_ref, tail_ref, da0_ref, db0_ref, da1_ref, db1_ref, out_ref):
    tail = tail_ref[...].astype(jnp.float32)
    groups = hidden_ref.shape[0]
    weight, hidden = [], []
    for e in range(2):
        weight.append(tail[:, 3 * e : 3 * e + 1] + tail[:, 3 * e + 1 : 3 * e + 2] + tail[:, 3 * e + 2 : 3 * e + 3])
        hidden.append(
            jnp.concatenate([hidden_ref[j, :, 128 * e : 128 * e + 128] for j in range(groups)], axis=1)
        )
    for side, (a_ref, b_ref) in enumerate(((da0_ref, db0_ref), (da1_ref, db1_ref))):
        total = 0.0
        for e, d_ref in enumerate((a_ref, b_ref)):
            y = jnp.dot(hidden[e], d_ref[...], preferred_element_type=jnp.float32)
            total = total + weight[e] * y.astype(jnp.bfloat16).astype(jnp.float32)
        where = half_ref[0] if side == 0 else 1 - half_ref[0]
        out_ref[where] = total.astype(jnp.bfloat16)


def down(half, hidden, tail, da0, db0, da1, db1):
    count, width = hidden.shape[1], da0.shape[1]
    vmem = pl.BlockSpec(memory_space=pltpu.VMEM)
    return pl.pallas_call(
        down_kernel,
        in_specs=[pl.BlockSpec(memory_space=pltpu.SMEM)] + [vmem] * 6,
        out_specs=vmem,
        out_shape=jax.ShapeDtypeStruct((2, count, width), jnp.bfloat16),
        name="down",
    )(half, hidden, tail, da0, db0, da1, db1)


def combine_tail(ids, comb, core, half):
    rows, experts = ids.shape[0] // 2, 32
    ids = jnp.where(half == 0, ids[:rows], ids[rows:])
    comb = jnp.where(half == 0, comb[:rows], comb[rows:])
    hit = ids[:, :, None] == jnp.arange(experts, dtype=jnp.int32)[None, None, :]
    dense = jnp.sum(jnp.where(hit, comb[:, :, None], 0.0), axis=1)
    dense = jnp.transpose(dense.reshape(rows, experts // 2, 2), (1, 0, 2))
    pair = jnp.where(core == 0, dense, dense[:, :, ::-1])
    high = lax.reduce_precision(pair, 8, 7)
    middle = lax.reduce_precision(pair - high, 8, 7)
    low = lax.reduce_precision(pair - high - middle, 8, 7)
    pieces = jnp.stack([high, middle, low], axis=3).reshape(experts // 2, rows, 6)
    return jnp.pad(pieces.astype(jnp.bfloat16), ((0, 0), (0, 0), (0, PAD - 6)))


def per_device(tokens, ids, comb, w_in, w_down):
    core, half = lax.axis_index("c"), lax.axis_index("zl")
    half_arr = half.astype(jnp.int32).reshape(1)
    swap = ((0, 1), (1, 0))
    w_in, w_down = w_in[0], w_down[0]
    rows, feats = tokens.shape[0] // 2, tokens.shape[1]
    depth = w_in.shape[0]

    with jax.named_scope("weights_near"):
        wa0, da0 = w_in, w_down
        wb0 = lax.ppermute(w_in, "c", swap)
        db0 = lax.ppermute(w_down, "c", swap)
    with jax.named_scope("weights_z"):
        wa1 = lax.ppermute(w_in, "zl", swap)
        da1 = lax.ppermute(w_down, "zl", swap)
    with jax.named_scope("weights_far"):
        wb1 = lax.ppermute(wa1, "c", swap)
        db1 = lax.ppermute(da1, "c", swap)

    with jax.named_scope("tokens_z"):
        pieces = jnp.broadcast_to(tokens.reshape(1, 2, rows, feats), (8, 2, rows, feats))
        pieces = lax.all_to_all(pieces.reshape(16, rows, feats), ("zh", "zl"), 0, 0, tiled=True)
        whole = jnp.transpose(pieces, (1, 0, 2)).reshape(rows, depth)
    with jax.named_scope("tokens_xy"):
        tail = combine_tail(ids, comb, core, half)
        sent = jnp.concatenate([jnp.broadcast_to(whole[None], (16, rows, depth)), tail], axis=2)
        got = lax.all_to_all(sent, XY, 0, 0, tiled=True).reshape(16 * rows, depth + PAD)
    hidden = gate_up(half_arr, got, wa0, wb0, wa1, wb1, depth)
    with jax.named_scope("hidden_z"):
        hidden = lax.all_gather(hidden, "zh")
    out = down(half_arr, hidden, got[:, depth:], da0, db0, da1, db1)
    with jax.named_scope("return"):
        back = lax.all_to_all(out.reshape(32, rows, feats), ("zl",) + XY, 0, 0, tiled=True)
        total = jnp.sum(back.reshape(2, 16, rows, feats).astype(jnp.float32), axis=1)
    return total.reshape(2 * rows, feats).astype(jnp.bfloat16)


def solution(mesh):
    fine = Mesh(mesh.devices.reshape(4, 4, 2, 8, 2), ("x", "y", "c", "zh", "zl"))
    e, t = ("x", "y", "c"), ("zh", "zl")
    in_specs = (P(e, t), P(e, None), P(e, None), P(e, None, t), P(e, None, t))
    return jax.shard_map(per_device, mesh=fine, in_specs=in_specs, out_specs=P(e, t), check_vma=False)
```

```python
import jax
import jax.numpy as jnp
from jax import lax
from jax.experimental import pallas as pl
from jax.experimental.pallas import tpu as pltpu
from jax.sharding import Mesh, PartitionSpec as P


XY = ("x", "y")
PAD = 128
HOPS = (0, 7, 1, 6, 2, 5, 3, 4)


def gate_up_kernel(half_ref, rows_ref, wa0_ref, wb0_ref, wa1_ref, wb1_ref, out_ref, acc_ref):
    step = pl.program_id(0)

    @pl.when(step == 0)
    def _():
        acc_ref[...] = jnp.zeros_like(acc_ref)

    weights = jnp.concatenate([wa0_ref[...], wa1_ref[...], wb0_ref[...], wb1_ref[...]], axis=1)
    acc_ref[...] += jnp.dot(rows_ref[...], weights, preferred_element_type=jnp.float32)

    @pl.when(step == pl.num_programs(0) - 1)
    def _():
        lane = lax.broadcasted_iota(jnp.int32, (rows_ref.shape[0], 128), 1)
        low = lane < 64
        first = jnp.where(low, 0, 1) == half_ref[0]

        def hidden(at):
            value = acc_ref[:, at : at + 128]
            turned = pltpu.roll(value, 64, 1)
            gate = jnp.where(low, value, turned)
            up = jnp.where(low, turned, value)
            return gate / (1.0 + jnp.exp(-gate)) * up

        for e in range(2):
            both = jnp.where(first, hidden(256 * e), hidden(256 * e + 128))
            out_ref[:, 128 * e : 128 * e + 128] = both.astype(jnp.bfloat16)


def gate_up(half, rows, wa0, wb0, wa1, wb1, depth):
    count, chunk = rows.shape[0], 1024
    w_spec = pl.BlockSpec((chunk, 128), lambda k: (k, 0))
    return pl.pallas_call(
        gate_up_kernel,
        grid=(depth // chunk,),
        in_specs=[
            pl.BlockSpec(memory_space=pltpu.SMEM),
            pl.BlockSpec((count, chunk), lambda k: (0, k)),
            w_spec,
            w_spec,
            w_spec,
            w_spec,
        ],
        out_specs=pl.BlockSpec((count, 256), lambda k: (0, 0)),
        out_shape=jax.ShapeDtypeStruct((count, 256), jnp.bfloat16),
        scratch_shapes=[pltpu.VMEM((count, 512), jnp.float32)],
        name="gate_up",
    )(half, rows, wa0, wb0, wa1, wb1)


def down_kernel(place_ref, h0, h1, h2, h3, h4, h5, h6, h7, tail_ref, da0_ref, db0_ref, da1_ref, db1_ref, out_ref):
    tail = tail_ref[...].astype(jnp.float32)
    parts = (h0, h1, h2, h3, h4, h5, h6, h7)
    weight, hidden = [], []
    for e in range(2):
        weight.append(tail[:, 3 * e : 3 * e + 1] + tail[:, 3 * e + 1 : 3 * e + 2] + tail[:, 3 * e + 2 : 3 * e + 3])
        hidden.append(jnp.concatenate([part[:, 128 * e : 128 * e + 128] for part in parts], axis=1))

    def rolled(d_ref):
        starts = [pl.multiple_of(lax.rem(place_ref[1] + by, 8) * 128, 128) for by in HOPS]
        return jnp.concatenate([d_ref[:, pl.ds(start, 128)] for start in starts], axis=1)

    for side, (a_ref, b_ref) in enumerate(((da0_ref, db0_ref), (da1_ref, db1_ref))):
        total = 0.0
        for e, d_ref in enumerate((a_ref, b_ref)):
            y = lax.dot_general(hidden[e], rolled(d_ref), (((1,), (1,)), ((), ())), preferred_element_type=jnp.float32)
            total = total + weight[e] * y.astype(jnp.bfloat16).astype(jnp.float32)
        where = place_ref[0] if side == 0 else 1 - place_ref[0]
        out_ref[where] = total.astype(jnp.bfloat16)


def down(place, parts, tail, da0, db0, da1, db1):
    count, width = parts[0].shape[0], da0.shape[0]
    vmem = pl.BlockSpec(memory_space=pltpu.VMEM)
    return pl.pallas_call(
        down_kernel,
        in_specs=[pl.BlockSpec(memory_space=pltpu.SMEM)] + [vmem] * 13,
        out_specs=vmem,
        out_shape=jax.ShapeDtypeStruct((2, count, width), jnp.bfloat16),
        name="down",
    )(place, *parts, tail, da0, db0, da1, db1)


def ring_gather(shard):
    left = tuple((j, (j + 1) % 8) for j in range(8))
    right = tuple((j, (j - 1) % 8) for j in range(8))
    parts, ahead, behind = [shard], shard, shard
    for step in range(4):
        ahead = lax.ppermute(ahead, "zh", left)
        parts.append(ahead)
        if step < 3:
            behind = lax.ppermute(behind, "zh", right)
            parts.append(behind)
    return parts


def combine_tail(ids, comb, core, half):
    rows, experts = ids.shape[0] // 2, 32
    ids = jnp.where(half == 0, ids[:rows], ids[rows:])
    comb = jnp.where(half == 0, comb[:rows], comb[rows:])
    hit = ids[:, :, None] == jnp.arange(experts, dtype=jnp.int32)[None, None, :]
    dense = jnp.sum(jnp.where(hit, comb[:, :, None], 0.0), axis=1)
    dense = jnp.transpose(dense.reshape(rows, experts // 2, 2), (1, 0, 2))
    pair = jnp.where(core == 0, dense, dense[:, :, ::-1])
    high = lax.reduce_precision(pair, 8, 7)
    middle = lax.reduce_precision(pair - high, 8, 7)
    low = lax.reduce_precision(pair - high - middle, 8, 7)
    pieces = jnp.stack([high, middle, low], axis=3).reshape(experts // 2, rows, 6)
    return jnp.pad(pieces.astype(jnp.bfloat16), ((0, 0), (0, 0), (0, PAD - 6)))


def layer(tokens, ids, comb, w_in, w_down):
    core, half = lax.axis_index("c"), lax.axis_index("zl")
    place = jnp.stack([half, lax.axis_index("zh")]).astype(jnp.int32)
    swap = ((0, 1), (1, 0))
    w_in, w_down = w_in[0], w_down[0].T
    rows, feats = tokens.shape[0] // 2, tokens.shape[1]
    depth = w_in.shape[0]

    wa0, da0 = w_in, w_down
    wb0 = lax.ppermute(w_in, "c", swap)
    db0 = lax.ppermute(w_down, "c", swap)
    wa1 = lax.ppermute(w_in, "zl", swap)
    da1 = lax.ppermute(w_down, "zl", swap)
    wb1 = lax.ppermute(wa1, "c", swap)
    db1 = lax.ppermute(da1, "c", swap)

    pieces = jnp.broadcast_to(tokens.reshape(1, 2, rows, feats), (8, 2, rows, feats))
    pieces = lax.all_to_all(pieces.reshape(16, rows, feats), ("zh", "zl"), 0, 0, tiled=True)
    whole = jnp.transpose(pieces, (1, 0, 2)).reshape(rows, depth)
    tail = combine_tail(ids, comb, core, half)
    sent = jnp.concatenate([jnp.broadcast_to(whole[None], (16, rows, depth)), tail], axis=2)
    got = lax.all_to_all(sent, XY, 0, 0, tiled=True).reshape(16 * rows, depth + PAD)
    hidden = gate_up(place, got, wa0, wb0, wa1, wb1, depth)
    parts = ring_gather(hidden)
    out = down(place, parts, got[:, depth:], da0, db0, da1, db1)
    back = lax.all_to_all(out.reshape(32, rows, feats), ("zl",) + XY, 0, 0, tiled=True)
    total = jnp.sum(back.reshape(2, 16, rows, feats).astype(jnp.float32), axis=1)
    return total.reshape(2 * rows, feats).astype(jnp.bfloat16)


def solution(mesh):
    fine = Mesh(mesh.devices.reshape(4, 4, 2, 8, 2), ("x", "y", "c", "zh", "zl"))
    e, t = ("x", "y", "c"), ("zh", "zl")
    in_specs = (P(e, t), P(e, None), P(e, None), P(e, None, t), P(e, None, t))
    return jax.shard_map(layer, mesh=fine, in_specs=in_specs, out_specs=P(e, t), check_vma=False)
```

```python
import jax
import jax.numpy as jnp
from jax import lax
from jax.experimental import pallas as pl
from jax.experimental.pallas import tpu as pltpu
from jax.sharding import Mesh, PartitionSpec as P


XY = ("x", "y")
PAD = 128
MAIN = 240


def gate_up_kernel(half_ref, rows_ref, wa0_ref, wb0_ref, wa1_ref, wb1_ref, main_ref, rest_ref, acc_ref):
    step = pl.program_id(0)

    @pl.when(step == 0)
    def _():
        acc_ref[...] = jnp.zeros_like(acc_ref)

    weights = jnp.concatenate([wa0_ref[...], wa1_ref[...], wb0_ref[...], wb1_ref[...]], axis=1)
    acc_ref[...] += jnp.dot(rows_ref[...], weights, preferred_element_type=jnp.float32)

    @pl.when(step == pl.num_programs(0) - 1)
    def _():
        lane = lax.broadcasted_iota(jnp.int32, (rows_ref.shape[0], 128), 1)
        low = lane < 64
        first = jnp.where(low, 0, 1) == half_ref[0]

        def hidden(at):
            value = acc_ref[:, at : at + 128]
            turned = pltpu.roll(value, 64, 1)
            gate = jnp.where(low, value, turned)
            up = jnp.where(low, turned, value)
            return gate / (1.0 + jnp.exp(-gate)) * up

        for e in range(2):
            both = jnp.where(first, hidden(256 * e), hidden(256 * e + 128))
            both = both.astype(jnp.bfloat16)
            main_ref[:, 128 * e : 128 * e + 128] = both[:MAIN]
            for j in range(rest_ref.shape[0]):
                rest_ref[j, :, 128 * e : 128 * e + 128] = both[MAIN:]


def gate_up(half, rows, wa0, wb0, wa1, wb1, depth):
    count, chunk = rows.shape[0], 1024
    w_spec = pl.BlockSpec((chunk, 128), lambda k: (k, 0))
    return pl.pallas_call(
        gate_up_kernel,
        grid=(depth // chunk,),
        in_specs=[
            pl.BlockSpec(memory_space=pltpu.SMEM),
            pl.BlockSpec((count, chunk), lambda k: (0, k)),
            w_spec,
            w_spec,
            w_spec,
            w_spec,
        ],
        out_specs=(
            pl.BlockSpec((MAIN, 256), lambda k: (0, 0)),
            pl.BlockSpec((8, count - MAIN, 256), lambda k: (0, 0, 0)),
        ),
        out_shape=(
            jax.ShapeDtypeStruct((MAIN, 256), jnp.bfloat16),
            jax.ShapeDtypeStruct((8, count - MAIN, 256), jnp.bfloat16),
        ),
        scratch_shapes=[pltpu.VMEM((count, 512), jnp.float32)],
        name="gate_up",
    )(half, rows, wa0, wb0, wa1, wb1)


def down_kernel(place_ref, main_ref, rest_ref, tail_ref, da0_ref, db0_ref, da1_ref, db1_ref, out_ref):
    tail = tail_ref[...].astype(jnp.float32)
    weight, hidden = [], []
    for e in range(2):
        weight.append(tail[:, 3 * e : 3 * e + 1] + tail[:, 3 * e + 1 : 3 * e + 2] + tail[:, 3 * e + 2 : 3 * e + 3])
        pieces = [
            jnp.concatenate([ref[j, :, 128 * e : 128 * e + 128] for ref in (main_ref, rest_ref)], axis=0)
            for j in range(8)
        ]
        hidden.append(jnp.concatenate(pieces, axis=1))
    for side, (a_ref, b_ref) in enumerate(((da0_ref, db0_ref), (da1_ref, db1_ref))):
        total = 0.0
        for e, d_ref in enumerate((a_ref, b_ref)):
            y = lax.dot_general(hidden[e], d_ref[...], (((1,), (1,)), ((), ())), preferred_element_type=jnp.float32)
            total = total + weight[e] * y.astype(jnp.bfloat16).astype(jnp.float32)
        where = place_ref[0] if side == 0 else 1 - place_ref[0]
        out_ref[where] = total.astype(jnp.bfloat16)


def down(place, main, rest, got, at, da0, db0, da1, db1):
    count, width = main.shape[1] + rest.shape[1], da0.shape[0]
    vmem = pl.BlockSpec(memory_space=pltpu.VMEM)
    return pl.pallas_call(
        down_kernel,
        grid=(1,),
        in_specs=[pl.BlockSpec(memory_space=pltpu.SMEM), vmem, vmem]
        + [pl.BlockSpec((count, PAD), lambda i: (0, at // PAD))]
        + [vmem] * 4,
        out_specs=pl.BlockSpec((2, count, width), lambda i: (0, 0, 0)),
        out_shape=jax.ShapeDtypeStruct((2, count, width), jnp.bfloat16),
        name="down",
    )(place, main, rest, got, da0, db0, da1, db1)


def combine_tail(ids, comb, core, half):
    rows, experts = ids.shape[0] // 2, 32
    ids = jnp.where(half == 0, ids[:rows], ids[rows:])
    comb = jnp.where(half == 0, comb[:rows], comb[rows:])
    hit = ids[:, :, None] == jnp.arange(experts, dtype=jnp.int32)[None, None, :]
    dense = jnp.sum(jnp.where(hit, comb[:, :, None], 0.0), axis=1)
    dense = jnp.transpose(dense.reshape(rows, experts // 2, 2), (1, 0, 2))
    pair = jnp.where(core == 0, dense, dense[:, :, ::-1])
    high = lax.reduce_precision(pair, 8, 7)
    middle = lax.reduce_precision(pair - high, 8, 7)
    low = lax.reduce_precision(pair - high - middle, 8, 7)
    pieces = jnp.stack([high, middle, low], axis=3).reshape(experts // 2, rows, 6)
    return jnp.pad(pieces.astype(jnp.bfloat16), ((0, 0), (0, 0), (0, PAD - 6)))


def layer(tokens, ids, comb, w_in, w_down):
    core, half = lax.axis_index("c"), lax.axis_index("zl")
    place = jnp.stack([half, lax.axis_index("zh")]).astype(jnp.int32)
    swap = ((0, 1), (1, 0))
    w_in, w_down = w_in[0], w_down[0].T
    rows, feats = tokens.shape[0] // 2, tokens.shape[1]
    depth = w_in.shape[0]

    wa0, da0 = w_in, w_down
    wb0 = lax.ppermute(w_in, "c", swap)
    db0 = lax.ppermute(w_down, "c", swap)
    wa1 = lax.ppermute(w_in, "zl", swap)
    da1 = lax.ppermute(w_down, "zl", swap)
    wb1 = lax.ppermute(wa1, "c", swap)
    db1 = lax.ppermute(da1, "c", swap)

    pieces = jnp.broadcast_to(tokens.reshape(1, 2, rows, feats), (8, 2, rows, feats))
    pieces = lax.all_to_all(pieces.reshape(16, rows, feats), ("zh", "zl"), 0, 0, tiled=True)
    whole = jnp.transpose(pieces, (1, 0, 2)).reshape(rows, depth)
    tail = combine_tail(ids, comb, core, half)
    sent = jnp.concatenate([jnp.broadcast_to(whole[None], (16, rows, depth)), tail], axis=2)
    got = lax.all_to_all(sent, XY, 0, 0, tiled=True).reshape(16 * rows, depth + PAD)
    main, rest = gate_up(place, got, wa0, wb0, wa1, wb1, depth)
    rest = lax.all_to_all(rest, "zh", 0, 0, tiled=True)
    main = lax.all_gather(main, "zh")
    out = down(place, main, rest, got, depth, da0, db0, da1, db1)
    back = lax.all_to_all(out.reshape(32, rows, feats), ("zl",) + XY, 0, 0, tiled=True)
    total = jnp.sum(back.reshape(2, 16, rows, feats).astype(jnp.float32), axis=1)
    return total.reshape(2 * rows, feats).astype(jnp.bfloat16)


def solution(mesh):
    fine = Mesh(mesh.devices.reshape(4, 4, 2, 8, 2), ("x", "y", "c", "zh", "zl"))
    e, t = ("x", "y", "c"), ("zh", "zl")
    in_specs = (P(e, t), P(e, None), P(e, None), P(e, None, t), P(e, None, t))
    return jax.shard_map(layer, mesh=fine, in_specs=in_specs, out_specs=P(e, t), check_vma=False)
```

```python
import jax
import jax.numpy as jnp
from jax import lax
from jax.experimental import pallas as pl
from jax.experimental.pallas import tpu as pltpu
from jax.sharding import Mesh, PartitionSpec as P


XY = ("x", "y")
PAD = 128
HOPS = (0, 7, 1, 6, 2, 5, 3, 4)


def gate_up_kernel(half_ref, rows_ref, wa0_ref, wa1_ref, wb0_ref, wb1_ref, out_ref, rows_buf, w_buf, acc_ref, sems):
    depth = wa0_ref.shape[0]
    chunks = sems.shape[0]
    chunk = depth // chunks

    def copies(k):
        span = pl.ds(k * chunk, chunk)
        yield pltpu.make_async_copy(rows_ref.at[:, span], rows_buf.at[:, span], sems.at[k, 0])
        for i, w_ref in enumerate((wa0_ref, wa1_ref, wb0_ref, wb1_ref)):
            yield pltpu.make_async_copy(w_ref.at[span, :], w_buf.at[span, pl.ds(128 * i, 128)], sems.at[k, i + 1])

    for k in range(chunks):
        for copy in copies(k):
            copy.start()
    for k in range(chunks):
        for copy in copies(k):
            copy.wait()
        span = pl.ds(k * chunk, chunk)
        part = jnp.dot(rows_buf[:, span], w_buf[span, :], preferred_element_type=jnp.float32)
        acc_ref[...] = part if k == 0 else acc_ref[...] + part

    lane = lax.broadcasted_iota(jnp.int32, (rows_ref.shape[0], 128), 1)
    low = lane < 64
    first = jnp.where(low, 0, 1) == half_ref[0]

    def hidden(at):
        value = acc_ref[:, at : at + 128]
        turned = pltpu.roll(value, 64, 1)
        gate = jnp.where(low, value, turned)
        up = jnp.where(low, turned, value)
        return gate / (1.0 + jnp.exp(-gate)) * up

    for e in range(2):
        both = jnp.where(first, hidden(256 * e), hidden(256 * e + 128))
        out_ref[:, 128 * e : 128 * e + 128] = both.astype(jnp.bfloat16)


def gate_up(half, rows, wa0, wa1, wb0, wb1):
    count, depth = rows.shape[0], wa0.shape[0]
    return pl.pallas_call(
        gate_up_kernel,
        in_specs=[pl.BlockSpec(memory_space=pltpu.SMEM)] + [pl.BlockSpec(memory_space=pl.ANY)] * 5,
        out_specs=pl.BlockSpec(memory_space=pltpu.VMEM),
        out_shape=jax.ShapeDtypeStruct((count, 256), jnp.bfloat16),
        scratch_shapes=[
            pltpu.VMEM((count, depth), jnp.bfloat16),
            pltpu.VMEM((depth, 512), jnp.bfloat16),
            pltpu.VMEM((count, 512), jnp.float32),
            pltpu.SemaphoreType.DMA((7, 5)),
        ],
        name="gate_up",
    )(half, rows, wa0, wa1, wb0, wb1)


def down_kernel(place_ref, h0_ref, h1, h2, h3, h4, h5, h6, h7, rows_ref, da0_ref, db0_ref, da1_ref, db1_ref, out_ref, d_buf, h_buf, tail_buf, sems):
    copies = [pltpu.make_async_copy(ref, d_buf.at[i], sems.at[i]) for i, ref in enumerate((da0_ref, db0_ref, da1_ref))]
    own_copy = pltpu.make_async_copy(h0_ref, h_buf, sems.at[3])
    tail_copy = pltpu.make_async_copy(rows_ref.at[:, pl.ds(rows_ref.shape[1] - PAD, PAD)], tail_buf, sems.at[4])
    for copy in (own_copy, tail_copy, *copies):
        copy.start()
    own_copy.wait()
    parts = (h_buf, h1, h2, h3, h4, h5, h6, h7)
    hidden = [jnp.concatenate([part[:, 128 * e : 128 * e + 128] for part in parts], axis=1) for e in range(2)]
    starts = [pl.multiple_of(lax.rem(place_ref[1] + by, 8) * 128, 128) for by in HOPS]
    tail_copy.wait()
    tail = tail_buf[...].astype(jnp.float32)
    weight = [
        tail[:, 3 * e : 3 * e + 1] + tail[:, 3 * e + 1 : 3 * e + 2] + tail[:, 3 * e + 2 : 3 * e + 3] for e in range(2)
    ]
    for side in range(2):
        total = 0.0
        for e in range(2):
            i = 2 * side + e
            if i < 3:
                copies[i].wait()
            d_ref = d_buf.at[i] if i < 3 else db1_ref
            rolled = jnp.concatenate([d_ref[:, pl.ds(start, 128)] for start in starts], axis=1)
            y = lax.dot_general(hidden[e], rolled, (((1,), (1,)), ((), ())), preferred_element_type=jnp.float32)
            total = total + weight[e] * y.astype(jnp.bfloat16).astype(jnp.float32)
        where = place_ref[0] if side == 0 else 1 - place_ref[0]
        out_ref[where] = total.astype(jnp.bfloat16)


def down(place, parts, rows, da0, db0, da1, db1):
    count, width = parts[0].shape[0], da0.shape[0]
    vmem, anywhere = pl.BlockSpec(memory_space=pltpu.VMEM), pl.BlockSpec(memory_space=pl.ANY)
    *parts, db1 = [parts[0]] + [pltpu.with_memory_space_constraint(a, pltpu.VMEM) for a in (*parts[1:], db1)]
    return pl.pallas_call(
        down_kernel,
        in_specs=[pl.BlockSpec(memory_space=pltpu.SMEM)] + [anywhere] + [vmem] * 7 + [anywhere] * 4 + [vmem],
        out_specs=vmem,
        out_shape=jax.ShapeDtypeStruct((2, count, width), jnp.bfloat16),
        scratch_shapes=[
            pltpu.VMEM((3, width, da0.shape[1]), jnp.bfloat16),
            pltpu.VMEM((count, 256), jnp.bfloat16),
            pltpu.VMEM((count, PAD), jnp.bfloat16),
            pltpu.SemaphoreType.DMA((5,)),
        ],
        name="down",
    )(place, *parts, rows, da0, db0, da1, db1)


def ring_gather(shard):
    left = tuple((j, (j + 1) % 8) for j in range(8))
    right = tuple((j, (j - 1) % 8) for j in range(8))
    parts, ahead, behind = [shard], shard, shard
    for step in range(4):
        ahead = lax.ppermute(ahead, "zh", left)
        parts.append(ahead)
        if step < 3:
            behind = lax.ppermute(behind, "zh", right)
            parts.append(behind)
    return parts


def combine_tail(ids, comb, core, half):
    rows, experts = ids.shape[0] // 2, 32
    ids = jnp.where(half == 0, ids[:rows], ids[rows:])
    comb = jnp.where(half == 0, comb[:rows], comb[rows:])
    hit = ids[:, :, None] == jnp.arange(experts, dtype=jnp.int32)[None, None, :]
    dense = jnp.sum(jnp.where(hit, comb[:, :, None], 0.0), axis=1)
    dense = jnp.transpose(dense.reshape(rows, experts // 2, 2), (1, 0, 2))
    pair = jnp.where(core == 0, dense, dense[:, :, ::-1])
    high = lax.reduce_precision(pair, 8, 7)
    middle = lax.reduce_precision(pair - high, 8, 7)
    low = lax.reduce_precision(pair - high - middle, 8, 7)
    pieces = jnp.stack([high, middle, low], axis=3).reshape(experts // 2, rows, 6)
    return jnp.pad(pieces.astype(jnp.bfloat16), ((0, 0), (0, 0), (0, PAD - 6)))


def layer(tokens, ids, comb, w_in, w_down):
    core, half = lax.axis_index("c"), lax.axis_index("zl")
    place = jnp.stack([half, lax.axis_index("zh")]).astype(jnp.int32)
    swap = ((0, 1), (1, 0))
    w_in, w_down = w_in[0], w_down[0].T
    rows, feats = tokens.shape[0] // 2, tokens.shape[1]
    depth = w_in.shape[0]

    wa0, da0 = w_in, w_down
    wb0 = lax.ppermute(w_in, "c", swap)
    db0 = lax.ppermute(w_down, "c", swap)
    wa1 = lax.ppermute(w_in, "zl", swap)
    da1 = lax.ppermute(w_down, "zl", swap)
    wb1 = lax.ppermute(wa1, "c", swap)
    db1 = lax.ppermute(da1, "c", swap)

    pieces = jnp.broadcast_to(tokens.reshape(1, 2, rows, feats), (8, 2, rows, feats))
    pieces = lax.all_to_all(pieces.reshape(16, rows, feats), ("zh", "zl"), 0, 0, tiled=True)
    whole = jnp.transpose(pieces, (1, 0, 2)).reshape(rows, depth)
    tail = combine_tail(ids, comb, core, half)
    sent = jnp.concatenate([jnp.broadcast_to(whole[None], (16, rows, depth)), tail], axis=2)
    got = lax.all_to_all(sent, XY, 0, 0, tiled=True).reshape(16 * rows, depth + PAD)
    hidden = gate_up(place, got, wa0, wa1, wb0, wb1)
    parts = ring_gather(hidden)
    out = down(place, parts, got, da0, db0, da1, db1)
    back = lax.all_to_all(out.reshape(32, rows, feats), ("zl",) + XY, 0, 0, tiled=True)
    total = jnp.sum(back.reshape(2, 16, rows, feats).astype(jnp.float32), axis=1)
    return total.reshape(2 * rows, feats).astype(jnp.bfloat16)


def solution(mesh):
    fine = Mesh(mesh.devices.reshape(4, 4, 2, 8, 2), ("x", "y", "c", "zh", "zl"))
    e, t = ("x", "y", "c"), ("zh", "zl")
    in_specs = (P(e, t), P(e, None), P(e, None), P(e, None, t), P(e, None, t))
    return jax.shard_map(layer, mesh=fine, in_specs=in_specs, out_specs=P(e, t), check_vma=False)
```

```python
import jax
import jax.numpy as jnp
from jax import lax
from jax.experimental import pallas as pl
from jax.experimental.pallas import tpu as pltpu
from jax.sharding import Mesh, PartitionSpec as P


XY = ("x", "y")
PAD = 128
HOPS = (0, 7, 1, 6, 2, 5, 3, 4)


def gate_up_kernel(half_ref, rows_ref, wa0_ref, wa1_ref, wb0_ref, wb1_ref, out_ref, rows_buf, w_buf, acc_ref, sems):
    depth = wa0_ref.shape[0]
    chunks = sems.shape[0]
    chunk = depth // chunks

    def copies(k):
        span = pl.ds(k * chunk, chunk)
        yield pltpu.make_async_copy(rows_ref.at[:, span], rows_buf.at[:, span], sems.at[k, 0])
        for i, w_ref in enumerate((wa0_ref, wa1_ref, wb0_ref, wb1_ref)):
            yield pltpu.make_async_copy(w_ref.at[span, :], w_buf.at[span, pl.ds(128 * i, 128)], sems.at[k, i + 1])

    for k in range(chunks):
        for copy in copies(k):
            copy.start()
    for k in range(chunks):
        for copy in copies(k):
            copy.wait()
        span = pl.ds(k * chunk, chunk)
        part = jnp.dot(rows_buf[:, span], w_buf[span, :], preferred_element_type=jnp.float32)
        acc_ref[...] = part if k == 0 else acc_ref[...] + part

    lane = lax.broadcasted_iota(jnp.int32, (rows_ref.shape[0], 128), 1)
    low = lane < 64
    first = jnp.where(low, 0, 1) == half_ref[0]

    def hidden(at):
        value = acc_ref[:, at : at + 128]
        turned = pltpu.roll(value, 64, 1)
        gate = jnp.where(low, value, turned)
        up = jnp.where(low, turned, value)
        return gate / (1.0 + jnp.exp(-gate)) * up

    for e in range(2):
        both = jnp.where(first, hidden(256 * e), hidden(256 * e + 128))
        out_ref[:, 128 * e : 128 * e + 128] = both.astype(jnp.bfloat16)


def gate_up(half, rows, wa0, wa1, wb0, wb1):
    count, depth = rows.shape[0], wa0.shape[0]
    return pl.pallas_call(
        gate_up_kernel,
        in_specs=[pl.BlockSpec(memory_space=pltpu.SMEM)] + [pl.BlockSpec(memory_space=pl.ANY)] * 5,
        out_specs=pl.BlockSpec(memory_space=pltpu.VMEM),
        out_shape=pltpu.VMEM((count, 256), jnp.bfloat16),
        scratch_shapes=[
            pltpu.VMEM((count, depth), jnp.bfloat16),
            pltpu.VMEM((depth, 512), jnp.bfloat16),
            pltpu.VMEM((count, 512), jnp.float32),
            pltpu.SemaphoreType.DMA((7, 5)),
        ],
        name="gate_up",
    )(half, rows, wa0, wa1, wb0, wb1)


def down_kernel(place_ref, h0, h1, h2, h3, h4, h5, h6, h7, rows_ref, da0_ref, db0_ref, da1_ref, db1_ref, out_ref, d_buf, tail_buf, sems):
    copies = [pltpu.make_async_copy(ref, d_buf.at[i], sems.at[i]) for i, ref in enumerate((da0_ref, db0_ref, da1_ref))]
    tail_copy = pltpu.make_async_copy(rows_ref.at[:, pl.ds(rows_ref.shape[1] - PAD, PAD)], tail_buf, sems.at[3])
    for copy in (tail_copy, *copies):
        copy.start()
    parts = (h0, h1, h2, h3, h4, h5, h6, h7)
    hidden = [jnp.concatenate([part[:, 128 * e : 128 * e + 128] for part in parts], axis=1) for e in range(2)]
    starts = [pl.multiple_of(lax.rem(place_ref[1] + by, 8) * 128, 128) for by in HOPS]
    tail_copy.wait()
    tail = tail_buf[...].astype(jnp.float32)
    weight = [
        tail[:, 3 * e : 3 * e + 1] + tail[:, 3 * e + 1 : 3 * e + 2] + tail[:, 3 * e + 2 : 3 * e + 3] for e in range(2)
    ]
    for side in range(2):
        total = 0.0
        for e in range(2):
            i = 2 * side + e
            if i < 3:
                copies[i].wait()
            d_ref = d_buf.at[i] if i < 3 else db1_ref
            rolled = jnp.concatenate([d_ref[:, pl.ds(start, 128)] for start in starts], axis=1)
            y = lax.dot_general(hidden[e], rolled, (((1,), (1,)), ((), ())), preferred_element_type=jnp.float32)
            total = total + weight[e] * y.astype(jnp.bfloat16).astype(jnp.float32)
        where = place_ref[0] if side == 0 else 1 - place_ref[0]
        out_ref[where] = total.astype(jnp.bfloat16)


def down(place, parts, rows, da0, db0, da1, db1):
    count, width = parts[0].shape[0], da0.shape[0]
    vmem, anywhere = pl.BlockSpec(memory_space=pltpu.VMEM), pl.BlockSpec(memory_space=pl.ANY)
    *parts, db1 = [pltpu.with_memory_space_constraint(a, pltpu.VMEM) for a in (*parts, db1)]
    return pl.pallas_call(
        down_kernel,
        in_specs=[pl.BlockSpec(memory_space=pltpu.SMEM)] + [vmem] * 8 + [anywhere] * 4 + [vmem],
        out_specs=vmem,
        out_shape=jax.ShapeDtypeStruct((2, count, width), jnp.bfloat16),
        scratch_shapes=[
            pltpu.VMEM((3, width, da0.shape[1]), jnp.bfloat16),
            pltpu.VMEM((count, PAD), jnp.bfloat16),
            pltpu.SemaphoreType.DMA((4,)),
        ],
        name="down",
    )(place, *parts, rows, da0, db0, da1, db1)


def ring_gather(shard):
    left = tuple((j, (j + 1) % 8) for j in range(8))
    right = tuple((j, (j - 1) % 8) for j in range(8))
    parts, ahead, behind = [shard], shard, shard
    for step in range(4):
        ahead = lax.ppermute(ahead, "zh", left)
        parts.append(ahead)
        if step < 3:
            behind = lax.ppermute(behind, "zh", right)
            parts.append(behind)
    return parts


def combine_tail(ids, comb, core, half):
    rows, experts = ids.shape[0] // 2, 32
    ids = jnp.where(half == 0, ids[:rows], ids[rows:])
    comb = jnp.where(half == 0, comb[:rows], comb[rows:])
    hit = ids[:, :, None] == jnp.arange(experts, dtype=jnp.int32)[None, None, :]
    dense = jnp.sum(jnp.where(hit, comb[:, :, None], 0.0), axis=1)
    dense = jnp.transpose(dense.reshape(rows, experts // 2, 2), (1, 0, 2))
    pair = jnp.where(core == 0, dense, dense[:, :, ::-1])
    high = lax.reduce_precision(pair, 8, 7)
    middle = lax.reduce_precision(pair - high, 8, 7)
    low = lax.reduce_precision(pair - high - middle, 8, 7)
    pieces = jnp.stack([high, middle, low], axis=3).reshape(experts // 2, rows, 6)
    return jnp.pad(pieces.astype(jnp.bfloat16), ((0, 0), (0, 0), (0, PAD - 6)))


def layer(tokens, ids, comb, w_in, w_down):
    core, half = lax.axis_index("c"), lax.axis_index("zl")
    place = jnp.stack([half, lax.axis_index("zh")]).astype(jnp.int32)
    swap = ((0, 1), (1, 0))
    w_in, w_down = w_in[0], w_down[0].T
    rows, feats = tokens.shape[0] // 2, tokens.shape[1]
    depth = w_in.shape[0]

    wa0, da0 = w_in, w_down
    wb0 = lax.ppermute(w_in, "c", swap)
    db0 = lax.ppermute(w_down, "c", swap)
    wa1 = lax.ppermute(w_in, "zl", swap)
    da1 = lax.ppermute(w_down, "zl", swap)
    wb1 = lax.ppermute(wa1, "c", swap)
    db1 = lax.ppermute(da1, "c", swap)

    pieces = jnp.broadcast_to(tokens.reshape(1, 2, rows, feats), (8, 2, rows, feats))
    pieces = lax.all_to_all(pieces.reshape(16, rows, feats), ("zh", "zl"), 0, 0, tiled=True)
    whole = jnp.transpose(pieces, (1, 0, 2)).reshape(rows, depth)
    tail = combine_tail(ids, comb, core, half)
    sent = jnp.concatenate([jnp.broadcast_to(whole[None], (16, rows, depth)), tail], axis=2)
    got = lax.all_to_all(sent, XY, 0, 0, tiled=True).reshape(16 * rows, depth + PAD)
    hidden = gate_up(place, got, wa0, wa1, wb0, wb1)
    parts = ring_gather(hidden)
    out = down(place, parts, got, da0, db0, da1, db1)
    back = lax.all_to_all(out.reshape(32, rows, feats), ("zl",) + XY, 0, 0, tiled=True)
    total = jnp.sum(back.reshape(2, 16, rows, feats).astype(jnp.float32), axis=1)
    return total.reshape(2 * rows, feats).astype(jnp.bfloat16)


def solution(mesh):
    fine = Mesh(mesh.devices.reshape(4, 4, 2, 8, 2), ("x", "y", "c", "zh", "zl"))
    e, t = ("x", "y", "c"), ("zh", "zl")
    in_specs = (P(e, t), P(e, None), P(e, None), P(e, None, t), P(e, None, t))
    return jax.shard_map(layer, mesh=fine, in_specs=in_specs, out_specs=P(e, t), check_vma=False)
```

```python
import jax
import jax.numpy as jnp
from jax import lax
from jax.experimental import pallas as pl
from jax.experimental.pallas import tpu as pltpu
from jax.sharding import Mesh, PartitionSpec as P


XY = ("x", "y")
PAD = 128
HOPS = (0, 7, 1, 6, 2, 5, 3, 4)


def gate_up_kernel(half_ref, rows_ref, wa0_ref, wa1_ref, wb0_ref, wb1_ref, out_ref, rows_buf, w_buf, acc_ref, sems):
    depth = wa0_ref.shape[0]
    chunks = sems.shape[0]
    chunk = depth // chunks

    def copies(k):
        span = pl.ds(k * chunk, chunk)
        yield pltpu.make_async_copy(rows_ref.at[:, span], rows_buf.at[:, span], sems.at[k, 0])
        for i, w_ref in enumerate((wa0_ref, wa1_ref, wb0_ref, wb1_ref)):
            yield pltpu.make_async_copy(w_ref.at[span, :], w_buf.at[span, pl.ds(128 * i, 128)], sems.at[k, i + 1])

    for k in range(chunks):
        for copy in copies(k):
            copy.start()
    for k in range(chunks):
        for copy in copies(k):
            copy.wait()
        span = pl.ds(k * chunk, chunk)
        part = jnp.dot(rows_buf[:, span], w_buf[span, :], preferred_element_type=jnp.float32)
        acc_ref[...] = part if k == 0 else acc_ref[...] + part

    lane = lax.broadcasted_iota(jnp.int32, (rows_ref.shape[0], 128), 1)
    low = lane < 64
    first = jnp.where(low, 0, 1) == half_ref[0]

    def hidden(at):
        value = acc_ref[:, at : at + 128]
        turned = pltpu.roll(value, 64, 1)
        gate = jnp.where(low, value, turned)
        up = jnp.where(low, turned, value)
        return gate / (1.0 + jnp.exp(-gate)) * up

    for e in range(2):
        both = jnp.where(first, hidden(256 * e), hidden(256 * e + 128))
        out_ref[:, 128 * e : 128 * e + 128] = both.astype(jnp.bfloat16)


def gate_up(half, rows, wa0, wa1, wb0, wb1):
    count, depth = rows.shape[0], wa0.shape[0]
    return pl.pallas_call(
        gate_up_kernel,
        in_specs=[pl.BlockSpec(memory_space=pltpu.SMEM)] + [pl.BlockSpec(memory_space=pl.ANY)] * 5,
        out_specs=pl.BlockSpec(memory_space=pltpu.VMEM),
        out_shape=pltpu.VMEM((count, 256), jnp.bfloat16),
        scratch_shapes=[
            pltpu.VMEM((count, depth), jnp.bfloat16),
            pltpu.VMEM((depth, 512), jnp.bfloat16),
            pltpu.VMEM((count, 512), jnp.float32),
            pltpu.SemaphoreType.DMA((4, 5)),
        ],
        name="gate_up",
    )(half, rows, wa0, wa1, wb0, wb1)


def down_kernel(place_ref, h0, h1, h2, h3, h4, h5, h6, h7, rows_ref, da0_ref, db0_ref, da1_ref, db1_ref, out_ref, d_buf, tail_buf, sems):
    copies = [pltpu.make_async_copy(ref, d_buf.at[i], sems.at[i]) for i, ref in enumerate((da1_ref, db0_ref, da0_ref))]
    tail_copy = pltpu.make_async_copy(rows_ref.at[:, pl.ds(rows_ref.shape[1] - PAD, PAD)], tail_buf, sems.at[3])
    for copy in (tail_copy, *copies):
        copy.start()
    parts = (h0, h1, h2, h3, h4, h5, h6, h7)
    hidden = [jnp.concatenate([part[:, 128 * e : 128 * e + 128] for part in parts], axis=1) for e in range(2)]
    starts = [pl.multiple_of(lax.rem(place_ref[1] + by, 8) * 128, 128) for by in HOPS]
    tail_copy.wait()
    tail = tail_buf[...].astype(jnp.float32)
    weight = [
        tail[:, 3 * e : 3 * e + 1] + tail[:, 3 * e + 1 : 3 * e + 2] + tail[:, 3 * e + 2 : 3 * e + 3] for e in range(2)
    ]
    for side in (1, 0):
        total = 0.0
        for e in (1, 0):
            i = 2 * (1 - side) - e
            if i >= 0:
                copies[i].wait()
            d_ref = d_buf.at[i] if i >= 0 else db1_ref
            rolled = jnp.concatenate([d_ref[:, pl.ds(start, 128)] for start in starts], axis=1)
            y = lax.dot_general(hidden[e], rolled, (((1,), (1,)), ((), ())), preferred_element_type=jnp.float32)
            total = total + weight[e] * y.astype(jnp.bfloat16).astype(jnp.float32)
        where = place_ref[0] if side == 0 else 1 - place_ref[0]
        out_ref[where] = total.astype(jnp.bfloat16)


def down(place, parts, rows, da0, db0, da1, db1):
    count, width = parts[0].shape[0], da0.shape[0]
    vmem, anywhere = pl.BlockSpec(memory_space=pltpu.VMEM), pl.BlockSpec(memory_space=pl.ANY)
    *parts, db1 = [pltpu.with_memory_space_constraint(a, pltpu.VMEM) for a in (*parts, db1)]
    return pl.pallas_call(
        down_kernel,
        in_specs=[pl.BlockSpec(memory_space=pltpu.SMEM)] + [vmem] * 8 + [anywhere] * 4 + [vmem],
        out_specs=vmem,
        out_shape=pltpu.VMEM((2, count, width), jnp.bfloat16),
        scratch_shapes=[
            pltpu.VMEM((3, width, da0.shape[1]), jnp.bfloat16),
            pltpu.VMEM((count, PAD), jnp.bfloat16),
            pltpu.SemaphoreType.DMA((4,)),
        ],
        name="down",
    )(place, *parts, rows, da0, db0, da1, db1)


def ring_gather(shard):
    left = tuple((j, (j + 1) % 8) for j in range(8))
    right = tuple((j, (j - 1) % 8) for j in range(8))
    parts, ahead, behind = [shard], shard, shard
    for step in range(4):
        ahead = lax.ppermute(ahead, "zh", left)
        parts.append(ahead)
        if step < 3:
            behind = lax.ppermute(behind, "zh", right)
            parts.append(behind)
    return parts


def combine_tail(ids, comb, core, half):
    rows, experts = ids.shape[0] // 2, 32
    ids = jnp.where(half == 0, ids[:rows], ids[rows:])
    comb = jnp.where(half == 0, comb[:rows], comb[rows:])
    hit = ids[:, :, None] == jnp.arange(experts, dtype=jnp.int32)[None, None, :]
    dense = jnp.sum(jnp.where(hit, comb[:, :, None], 0.0), axis=1)
    dense = jnp.transpose(dense.reshape(rows, experts // 2, 2), (1, 0, 2))
    pair = jnp.where(core == 0, dense, dense[:, :, ::-1])
    high = lax.reduce_precision(pair, 8, 7)
    middle = lax.reduce_precision(pair - high, 8, 7)
    low = lax.reduce_precision(pair - high - middle, 8, 7)
    pieces = jnp.stack([high, middle, low], axis=3).reshape(experts // 2, rows, 6)
    return jnp.pad(pieces.astype(jnp.bfloat16), ((0, 0), (0, 0), (0, PAD - 6)))


def layer(tokens, ids, comb, w_in, w_down):
    core, half = lax.axis_index("c"), lax.axis_index("zl")
    place = jnp.stack([half, lax.axis_index("zh")]).astype(jnp.int32)
    swap = ((0, 1), (1, 0))
    w_in, w_down = w_in[0], w_down[0].T
    rows, feats = tokens.shape[0] // 2, tokens.shape[1]
    depth = w_in.shape[0]

    wa0, da0 = w_in, w_down
    wb0 = lax.ppermute(w_in, "c", swap)
    db0 = lax.ppermute(w_down, "c", swap)
    wa1 = lax.ppermute(w_in, "zl", swap)
    da1 = lax.ppermute(w_down, "zl", swap)
    wb1 = lax.ppermute(wa1, "c", swap)
    db1 = lax.ppermute(da1, "c", swap)

    pieces = jnp.broadcast_to(tokens.reshape(1, 2, rows, feats), (8, 2, rows, feats))
    pieces = lax.all_to_all(pieces.reshape(16, rows, feats), ("zh", "zl"), 0, 0, tiled=True)
    whole = jnp.transpose(pieces, (1, 0, 2)).reshape(rows, depth)
    tail = combine_tail(ids, comb, core, half)
    sent = jnp.concatenate([jnp.broadcast_to(whole[None], (16, rows, depth)), tail], axis=2)
    got = lax.all_to_all(sent, XY, 0, 0, tiled=True).reshape(16 * rows, depth + PAD)
    hidden = gate_up(place, got, wa0, wa1, wb0, wb1)
    parts = ring_gather(hidden)
    out = down(place, parts, got, da0, db0, da1, db1)
    back = lax.all_to_all(out.reshape(32, rows, feats), ("zl",) + XY, 0, 0, tiled=True)
    total = jnp.sum(back.reshape(2, 16, rows, feats).astype(jnp.float32), axis=1)
    return total.reshape(2 * rows, feats).astype(jnp.bfloat16)


def solution(mesh):
    fine = Mesh(mesh.devices.reshape(4, 4, 2, 8, 2), ("x", "y", "c", "zh", "zl"))
    e, t = ("x", "y", "c"), ("zh", "zl")
    in_specs = (P(e, t), P(e, None), P(e, None), P(e, None, t), P(e, None, t))
    return jax.shard_map(layer, mesh=fine, in_specs=in_specs, out_specs=P(e, t), check_vma=False)
```
